32 devices in a mesh: dp: 16 (over z, x, core), ctx: 2 (over y).
Axes of the slice: x: 2, y: 2, z: 4, core: 2. Of those that a mesh axis runs over, the one named last changes fastest.
Arguments:
- tokens: bfloat16 [16, 256, 1088], P('dp', 'ctx')
- attn_weight: float32 [4352, 1088], P(('dp', 'ctx'))
- up_weight: float32 [1088, 4352], P(None, ('dp', 'ctx')), may hold values from -0.1875 to 0.1875
- down_weight: float32 [4352, 1088], P(('dp', 'ctx')), may hold values from -0.09375 to 0.09375
- vectors: float32 [13056], P(('dp', 'ctx'))
- attn_moments: float32 [2, 4352, 1088], P(None, ('dp', 'ctx')), as said below
- up_moments: float32 [2, 1088, 4352], P(None, None, ('dp', 'ctx')), as said below
- down_moments: float32 [2, 4352, 1088], P(None, ('dp', 'ctx')), as said below
- vector_moments: float32 [2, 13056], P(None, ('dp', 'ctx')), as said below
- cotangent: bfloat16 [16, 256, 1088], P('dp', 'ctx'), may hold values from -0.0625 to 0.0625
Outputs:
- block_out: float32 [16, 256, 1088], P('dp', 'ctx')
- block_input_gradient: float32 [16, 256, 1088], P('dp', 'ctx')
- attn_grad: float32 [4352, 1088], P(('dp', 'ctx'))
- up_grad: float32 [1088, 4352], P(None, ('dp', 'ctx'))
- down_grad: float32 [4352, 1088], P(('dp', 'ctx'))
- vector_grad: float32 [13056], P(('dp', 'ctx'))
- attn_new: float32 [4352, 1088], P(('dp', 'ctx'))
- up_new: float32 [1088, 4352], P(None, ('dp', 'ctx'))
- down_new: float32 [4352, 1088], P(('dp', 'ctx'))
- vector_new: float32 [13056], P(('dp', 'ctx'))
- attn_moments_new: float32 [2, 4352, 1088], P(None, ('dp', 'ctx'))
- up_moments_new: float32 [2, 1088, 4352], P(None, None, ('dp', 'ctx'))
- down_moments_new: float32 [2, 4352, 1088], P(None, ('dp', 'ctx'))
- vector_moments_new: float32 [2, 13056], P(None, ('dp', 'ctx'))
The draws below stay inside these ranges and needn't reach their ends.
Inputs may be any that keep to these rules, and one draw needn't show every extreme that they name: `attn_moments`: the second moments are positive. `up_moments`: the second moments are positive. `down_moments`: the second moments are positive. `vector_moments`: the second moments are positive.
All inputs are finite; a program needn't handle non-finite values.
Results may differ from the reference program's by a relative error of at most 0.0075.
The reference program's roundings to bfloat16 on the way count: a program that leaves them out, or rounds other values in their place, can miss the bound.
Values may be sent and summed in bfloat16 or wider, within the bound.
No kernel may reach another device: no remote copies, remote signals or barrier semaphores. Data moves between devices by JAX's collectives and lax.ppermute only.
A program may use at most 192 MiB of HBM per device.

```python
import math
import jax
import jax.numpy as jnp
from jax import lax

D = 1088
H = 17
HD = 64
FF = 4352
LENGTH = 256
SEQS = 16
VEC = 13056


def moment_pair(key, extent, spread, lowest, highest):
    key_one, key_two = jax.random.split(key)
    mean_part = jnp.clip(jax.random.normal(key_one, extent, jnp.float32), -5.0, 5.0) * spread
    square_part = jnp.exp(jax.random.uniform(key_two, extent, jnp.float32, math.log(lowest), math.log(highest)))
    return jnp.stack([mean_part, square_part], 0)


def draw_tokens(key, part):
    key_one = jax.random.fold_in(jax.random.fold_in(key, 11), 0)
    drawn = jnp.clip(jax.random.normal(key_one, (SEQS, LENGTH, D), jnp.float32), -6.0, 6.0)
    return drawn.astype(jnp.bfloat16)


def draw_attn_weight(key, part):
    key_one = jax.random.fold_in(jax.random.fold_in(key, 23), 0)
    drawn = jnp.clip(jax.random.normal(key_one, (4 * D, D), jnp.float32), -4.0, 4.0)
    block_index = (jnp.arange(4 * D) // D)[:, None]
    scale_rows = jnp.where(block_index == 3, 12.0, 1.0) * D ** (-0.5)
    return drawn * scale_rows


def draw_vectors(key, part):
    drawn = jnp.clip(jax.random.normal(jax.random.fold_in(key, 37), (VEC,), jnp.float32), -4.0, 4.0)
    position = jnp.arange(VEC) % 12
    is_gain = (position == 0) | (position == 2)
    return jnp.where(is_gain, 1.0 + 0.15 * jnp.clip(drawn, -3.0, 3.0), 0.3 * drawn)


def draw_attn_moments(key, part):
    return moment_pair(jax.random.fold_in(key, 41), (4 * D, D), 0.3, 0.01, 1.0)


def draw_up_moments(key, part):
    return moment_pair(jax.random.fold_in(key, 43), (D, FF), 0.05, 0.001, 0.05)


def draw_down_moments(key, part):
    return moment_pair(jax.random.fold_in(key, 47), (FF, D), 0.08, 0.002, 0.1)


def draw_vector_moments(key, part):
    return moment_pair(jax.random.fold_in(key, 53), (VEC,), 0.5, 0.01, 3.0)


def block_levels(own_key, shape, cuts, smallest, top_value):
    def one(dim, blocks):
        heights = jax.random.uniform(jax.random.fold_in(jax.random.fold_in(own_key, 6), dim), (blocks,), jnp.float32, smallest / len(cuts), top_value / len(cuts))
        return jnp.repeat(jnp.exp(heights), shape[dim] // blocks).reshape((-1,) + (1,) * (len(shape) - dim - 1))

    loudness = one(*cuts[0])
    for cut in cuts[1:]:
        loudness = loudness * one(*cut)
    return loudness


def normal_values(own_key, dims, scale, limit, cuts=(), kind=jnp.bfloat16):
    values = scale * jax.random.normal(own_key, dims, jnp.float32)
    if cuts:
        values = values * block_levels(own_key, dims, cuts, -0.22, 0.18)
    return jnp.clip(values, -limit, limit).astype(kind)


def setup_inputs(seed: int = 0) -> dict:
    splits = jax.random.split(jax.random.key(seed), 11)
    return {
        "tokens": draw_tokens(jax.random.fold_in(splits[10], 71), 0),
        "attn_weight": draw_attn_weight(jax.random.fold_in(splits[10], 71), 0),
        "up_weight": normal_values(splits[2], (D, FF), D ** -0.5, 0.1875, ((1, 32),), jnp.float32),
        "down_weight": normal_values(splits[3], (FF, D), FF ** -0.5, 0.09375, ((0, 32),), jnp.float32),
        "vectors": draw_vectors(jax.random.fold_in(splits[10], 71), 0),
        "attn_moments": draw_attn_moments(jax.random.fold_in(splits[10], 71), 0),
        "up_moments": draw_up_moments(jax.random.fold_in(splits[10], 71), 0),
        "down_moments": draw_down_moments(jax.random.fold_in(splits[10], 71), 0),
        "vector_moments": draw_vector_moments(jax.random.fold_in(splits[10], 71), 0),
        "cotangent": normal_values(splits[9], (SEQS, LENGTH, D), 0.01, 0.0625, ((0, 16), (1, 2))),
    }


norm_eps = 1e-05
beta_one = 0.9
beta_two = 0.95
adam_eps = 1e-08
learn_rate = 0.06
decay_rate = 0.1
first_fix = 1.0 - 0.9 ** 5.0
second_fix = 1.0 - 0.95 ** 5.0
masked_fill = -1e+30

def gelu_pair(pre_act):
    cumulative = 0.5 * (1.0 + lax.erf(pre_act * 0.7071067811865476))
    density = jnp.exp(-0.5 * pre_act * pre_act) * 0.3989422804014327
    return (pre_act * cumulative, cumulative + pre_act * density)

def layer_norm_forward(resid, gain_vec, offset):
    center = resid - lax.optimization_barrier(jnp.mean(resid, axis=-1, keepdims=True))
    inv_std = lax.rsqrt(lax.optimization_barrier(jnp.mean(center * center, axis=-1, keepdims=True)) + norm_eps)
    normed = center * inv_std
    return (normed * gain_vec + offset, normed, inv_std)

def layer_norm_backward(grad_norm, gain_vec, normed, inv_std):
    scaled = grad_norm * gain_vec
    return inv_std * (scaled - lax.optimization_barrier(jnp.mean(scaled, axis=-1, keepdims=True)) - normed * lax.optimization_barrier(jnp.mean(scaled * normed, axis=-1, keepdims=True)))

def split_vectors(vector_vals, features):
    vector_table = vector_vals.reshape(features, 12)
    pieces = [vector_table[:, piece_index] for piece_index in range(8)]
    return pieces + [vector_table[:, 8:].reshape(4 * features)]

def join_vectors(pieces, unit_part, features):
    vector_table = jnp.concatenate([jnp.stack(pieces, axis=1), unit_part.reshape(features, 4)], axis=1)
    return vector_table.reshape(12 * features)

def adam_update(weight, moments, gradient, decay_factor):
    mean_new = beta_one * moments[0] + (1.0 - beta_one) * gradient
    square_new = beta_two * moments[1] + (1.0 - beta_two) * gradient * gradient
    update_dir = mean_new / first_fix / (jnp.sqrt(square_new / second_fix) + adam_eps)
    return (weight - learn_rate * (update_dir + decay_factor * weight), jnp.stack([mean_new, square_new], 0))

def reference(tokens, attn_weight, up_weight, down_weight, vectors, attn_moments, up_moments, down_moments, vector_moments, cotangent):
    features = D
    score_scale = HD ** (-0.5)
    attn_b = attn_weight.astype(jnp.bfloat16)
    up_b = up_weight.astype(jnp.bfloat16)
    down_b = down_weight.astype(jnp.bfloat16)
    vector_vals = lax.optimization_barrier(vectors.astype(jnp.bfloat16)).astype(jnp.float32)
    w_query = attn_b[0:features]
    w_key = attn_b[features:2 * features]
    w_value = attn_b[2 * features:3 * features]
    w_out = attn_b[3 * features:]
    first_norm_scale, first_norm_bias, second_norm_scale, second_norm_bias, bias_query, bias_value, bias_out, bias_down, bias_up = split_vectors(vector_vals, features)
    causal = jnp.arange(LENGTH)[:, None] >= jnp.arange(LENGTH)[None, :]

    def one_sequence(totals, seq_pair):
        seq_tokens, seq_cot = seq_pair
        residual_input = seq_tokens.astype(jnp.float32)
        final_layer_norm, first_normalized_input, first_inverse_deviation = layer_norm_forward(residual_input, first_norm_scale, first_norm_bias)
        norm_one = final_layer_norm.astype(jnp.bfloat16)
        queries = (jnp.dot(norm_one, w_query, preferred_element_type=jnp.float32) + bias_query).astype(jnp.bfloat16)
        key_rows = jnp.dot(norm_one, w_key, preferred_element_type=jnp.float32).astype(jnp.bfloat16)
        values = (jnp.dot(norm_one, w_value, preferred_element_type=jnp.float32) + bias_value).astype(jnp.bfloat16)
        query_heads = queries.reshape(LENGTH, H, HD).astype(jnp.float32)
        key_heads = key_rows.reshape(LENGTH, H, HD).astype(jnp.float32)
        value_heads = values.reshape(LENGTH, H, HD).astype(jnp.float32)
        scores = jnp.einsum('thd,shd->hts', query_heads, key_heads) * score_scale
        masked = jnp.where(causal, scores, masked_fill)
        row_max = lax.optimization_barrier(jnp.max(masked, axis=-1, keepdims=True))
        log_total = row_max + jnp.log(lax.optimization_barrier(jnp.sum(jnp.exp(masked - row_max), axis=-1, keepdims=True)))
        prob_f = jnp.where(causal, jnp.exp(scores - log_total), 0.0)
        attn_prob = prob_f.astype(jnp.bfloat16)
        context = jnp.einsum('hts,shd->thd', attn_prob.astype(jnp.float32), value_heads).reshape(LENGTH, features).astype(jnp.bfloat16)
        residual_middle = residual_input + jnp.dot(context, w_out, preferred_element_type=jnp.float32) + bias_out
        norm_input_gradient, second_normalized_input, second_inverse_deviation = layer_norm_forward(residual_middle, second_norm_scale, second_norm_bias)
        norm_two = norm_input_gradient.astype(jnp.bfloat16)
        pre_act = jnp.dot(norm_two, up_b, preferred_element_type=jnp.float32) + bias_up
        activated, act_slope = gelu_pair(pre_act)
        hidden_b = activated.astype(jnp.bfloat16)
        block_out = residual_middle + jnp.dot(hidden_b, down_b, preferred_element_type=jnp.float32) + bias_down
        final_output_gradient = seq_cot.astype(jnp.float32)
        preactivation_gradient = jnp.dot(seq_cot, down_b.T, preferred_element_type=jnp.float32) * act_slope
        grad_pre_b = preactivation_gradient.astype(jnp.bfloat16)
        second_layer_gradient = jnp.dot(grad_pre_b, up_b.T, preferred_element_type=jnp.float32)
        residual_gradient = final_output_gradient + layer_norm_backward(second_layer_gradient, second_norm_scale, second_normalized_input, second_inverse_deviation)
        grad_resid_b = residual_gradient.astype(jnp.bfloat16)
        grad_context = jnp.dot(grad_resid_b, w_out.T, preferred_element_type=jnp.float32).astype(jnp.bfloat16)
        context_heads = grad_context.reshape(LENGTH, H, HD).astype(jnp.float32)
        grad_prob = jnp.einsum('thd,shd->hts', context_heads, value_heads)
        row_delta = lax.optimization_barrier(jnp.sum(prob_f * grad_prob, axis=-1, keepdims=True))
        grad_score = (prob_f * (grad_prob - row_delta) * score_scale).astype(jnp.bfloat16).astype(jnp.float32)
        query_gradient = jnp.einsum('hts,shd->thd', grad_score, key_heads).reshape(LENGTH, features)
        grad_key = jnp.einsum('hts,thd->shd', grad_score, query_heads).reshape(LENGTH, features)
        value_gradient = jnp.einsum('hts,thd->shd', attn_prob.astype(jnp.float32), context_heads).reshape(LENGTH, features)
        grad_query_b = query_gradient.astype(jnp.bfloat16)
        grad_key_b = grad_key.astype(jnp.bfloat16)
        grad_value_b = value_gradient.astype(jnp.bfloat16)
        first_layer_gradient = jnp.dot(grad_query_b, w_query.T, preferred_element_type=jnp.float32) + jnp.dot(grad_key_b, w_key.T, preferred_element_type=jnp.float32) + jnp.dot(grad_value_b, w_value.T, preferred_element_type=jnp.float32)
        block_input_gradient = residual_gradient + layer_norm_backward(first_layer_gradient, first_norm_scale, first_normalized_input, first_inverse_deviation)
        attn_part = jnp.concatenate([jnp.dot(norm_one.T, grad_query_b, preferred_element_type=jnp.float32), jnp.dot(norm_one.T, grad_key_b, preferred_element_type=jnp.float32), jnp.dot(norm_one.T, grad_value_b, preferred_element_type=jnp.float32), jnp.dot(context.T, grad_resid_b, preferred_element_type=jnp.float32)], axis=0)
        up_part = jnp.dot(norm_two.T, grad_pre_b, preferred_element_type=jnp.float32)
        down_part = jnp.dot(hidden_b.T, seq_cot, preferred_element_type=jnp.float32)
        vector_shard_slice = join_vectors([lax.optimization_barrier(jnp.sum(first_layer_gradient * first_normalized_input, axis=0)), lax.optimization_barrier(jnp.sum(first_layer_gradient, axis=0)), lax.optimization_barrier(jnp.sum(second_layer_gradient * second_normalized_input, axis=0)), lax.optimization_barrier(jnp.sum(second_layer_gradient, axis=0)), lax.optimization_barrier(jnp.sum(query_gradient, axis=0)), lax.optimization_barrier(jnp.sum(value_gradient, axis=0)), lax.optimization_barrier(jnp.sum(residual_gradient, axis=0)), lax.optimization_barrier(jnp.sum(final_output_gradient, axis=0))], lax.optimization_barrier(jnp.sum(preactivation_gradient, axis=0)), features)
        new_totals = (totals[0] + attn_part, totals[1] + up_part, totals[2] + down_part, totals[3] + vector_shard_slice)
        return (new_totals, (block_out, block_input_gradient))
    start_totals = (jnp.zeros((4 * D, D), jnp.float32), jnp.zeros((D, FF), jnp.float32), jnp.zeros((FF, D), jnp.float32), jnp.zeros((VEC,), jnp.float32))
    totals, outputs = lax.scan(one_sequence, start_totals, (tokens, cotangent))
    block_out, block_input_gradient = outputs
    attn_grad, up_grad, down_grad, vector_grad = totals
    attn_new, attn_moments_new = adam_update(attn_weight, attn_moments, attn_grad, decay_rate)
    up_new, up_moments_new = adam_update(up_weight, up_moments, up_grad, decay_rate)
    down_new, down_moments_new = adam_update(down_weight, down_moments, down_grad, decay_rate)
    vector_new, vector_moments_new = adam_update(vectors, vector_moments, vector_grad, 0.0)
    return (block_out, block_input_gradient, attn_grad, up_grad, down_grad, vector_grad, attn_new, up_new, down_new, vector_new, attn_moments_new, up_moments_new, down_moments_new, vector_moments_new)
```

```python
import jax
import jax.numpy as jnp
from jax import lax
from jax.experimental import pallas as pl
from jax.experimental.pallas import tpu as pltpu
from jax.sharding import Mesh, PartitionSpec as P

H = 17
HD = 64
PLANE = ("x", "c", "ctx")

norm_eps = 1e-05
beta_one = 0.9
beta_two = 0.95
adam_eps = 1e-08
learn_rate = 0.06
decay_rate = 0.1
first_fix = 1.0 - 0.9**5.0
second_fix = 1.0 - 0.95**5.0
masked_fill = -1e30
score_scale = HD ** (-0.5)
bf16 = jnp.bfloat16
f32 = jnp.float32


def gelu_pair(pre_act):
    cumulative = 0.5 * (1.0 + lax.erf(pre_act * 0.7071067811865476))
    density = jnp.exp(-0.5 * pre_act * pre_act) * 0.3989422804014327
    return (pre_act * cumulative, cumulative + pre_act * density)


def layer_norm_forward(resid, gain_vec, offset):
    center = resid - jnp.mean(resid, axis=-1, keepdims=True)
    inv_std = lax.rsqrt(jnp.mean(center * center, axis=-1, keepdims=True) + norm_eps)
    normed = center * inv_std
    return (normed * gain_vec + offset, normed, inv_std)


def layer_norm_backward(grad_norm, gain_vec, normed, inv_std):
    scaled = grad_norm * gain_vec
    return inv_std * (
        scaled
        - jnp.mean(scaled, axis=-1, keepdims=True)
        - normed * jnp.mean(scaled * normed, axis=-1, keepdims=True)
    )


def product(left, right, left_dim, right_dim):
    return lax.dot_general(
        left, right, (((left_dim,), (right_dim,)), ((), ())), preferred_element_type=f32
    )


def adam_update(weight, moments, gradient, decay_factor):
    mean_new = beta_one * moments[0] + (1.0 - beta_one) * gradient
    square_new = beta_two * moments[1] + (1.0 - beta_two) * gradient * gradient
    update_dir = mean_new / first_fix / (jnp.sqrt(square_new / second_fix) + adam_eps)
    return (
        weight - learn_rate * (update_dir + decay_factor * weight),
        jnp.stack([mean_new, square_new], 0),
    )


def plane_bits():
    n_ctx = lax.axis_size("ctx")
    ctx_bits = [1 << b for b in range(n_ctx.bit_length() - 1)]
    return n_ctx, 2 * n_ctx, ctx_bits


def member_bits(slot):
    x_bit, c_bit, _ = plane_bits()
    low = slot % x_bit
    return low + (c_bit if slot & x_bit else 0) + (x_bit if slot & c_bit else 0)


def swap(piece, bit):
    members = 4 * lax.axis_size("ctx")
    return lax.ppermute(piece, PLANE, [(i, i ^ member_bits(bit)) for i in range(members)])


def assemble(parts, shape, index=None, lane_block=0):
    scal = jnp.zeros((1,), jnp.int32) if index is None else index.reshape(1)

    def kernel(scal_ref, *refs):
        out_ref = refs[len(parts)]
        for (slot, row, array), ref in zip(parts, refs):
            place = slot if index is None else scal_ref[0] ^ member_bits(slot)
            last = row + array.shape[0]
            if not lane_block:
                out_ref[place, row:last, :] = ref[...]
                continue
            for t in range(shape[0]):
                s = t ^ slot
                out_ref[place, row:last, t * lane_block : (t + 1) * lane_block] = ref[
                    :, s * lane_block : (s + 1) * lane_block
                ]

    def whole(array_shape):
        return pl.BlockSpec(array_shape, lambda i, s: (0,) * len(array_shape))

    return pl.pallas_call(
        kernel,
        out_shape=jax.ShapeDtypeStruct(shape, parts[0][2].dtype),
        grid_spec=pltpu.PrefetchScalarGridSpec(
            num_scalar_prefetch=1,
            grid=(1,),
            in_specs=[whole(array.shape) for _, _, array in parts],
            out_specs=whole(shape),
        ),
        name="assemble",
    )(scal, *[array for _, _, array in parts])


def plane_gather(piece, index=None, lane_block=0):
    x_bit, c_bit, ctx_bits = plane_bits()
    half = piece.shape[0] // 16 * 8
    shape = (4 * lax.axis_size("ctx"),) + piece.shape
    if len(ctx_bits) == 1:
        from_x, from_y, from_c = (swap(piece, x_bit), swap(piece, 1), swap(piece, c_bit))
        diag_low = swap(from_x[:half], 1)
        diag_high = swap(from_y[half:], x_bit)
        cx, cy = (swap(from_x, c_bit), swap(from_y, c_bit))
        c_low, c_high = (swap(diag_low, c_bit), swap(diag_high, c_bit))
        xy, xc, yc, xyc = (x_bit + 1, x_bit + c_bit, c_bit + 1, x_bit + c_bit + 1)
        parts = [(0, 0, piece), (1, 0, from_y), (c_bit, 0, from_c), (yc, 0, cy)]
        parts += [(x_bit, 0, from_x), (xy, 0, diag_low), (xy, half, diag_high), (xc, 0, cx)]
        parts += [(xyc, 0, c_low), (xyc, half, c_high)]
        return assemble(parts, shape, index, lane_block)
    offsets, whole = [0], piece[None]
    for bit in [x_bit] + ctx_bits + [c_bit]:
        whole = jnp.concatenate([whole, swap(whole, bit)], axis=0)
        offsets = offsets + [o ^ bit for o in offsets]
    order = [offsets.index(k) for k in range(len(offsets))]
    whole = jnp.concatenate([whole[o : o + 1] for o in order], axis=0)
    if lane_block:
        whole = jnp.stack(
            [
                whole[k].reshape(piece.shape[0], -1, lane_block)[:, [t ^ k for t in range(shape[0])]]
                for k in range(shape[0])
            ]
        ).reshape(shape)
    if index is None:
        return whole
    swapped = jnp.stack([whole[member_bits(k)] for k in range(shape[0])])
    return slots_to_members(swapped, index)


def plane_sum(left, right, right_dim, meanwhile=None):
    x_bit, c_bit, ctx_bits = plane_bits()
    count = 2 * c_bit
    rows = left.shape[0] // count
    middle = left.shape[0] // 2

    def send(array, bit):
        return swap(array.astype(bf16), bit)

    moved = send(product(left[middle:], right, 1, right_dim), c_bit)
    kept = product(left[:middle], right, 1, right_dim)
    extra = None
    if meanwhile is not None:
        extra = meanwhile()
        moved, kept, extra = lax.optimization_barrier((moved, kept, extra))

    def part(slot, first, last):
        at = slice(slot * rows + first, slot * rows + last)
        return kept[at] + moved[at].astype(f32)

    if len(ctx_bits) == 1:
        half = rows // 2
        diag = x_bit + 1
        low, high = (send(part(diag, 0, half), 1), send(part(diag, half, rows), x_bit))
        x_top, y_low = (send(part(x_bit, half, rows), x_bit), send(part(1, 0, half), 1))
        x_low = send(part(x_bit, 0, half) + low.astype(f32), x_bit)
        y_top = send(part(1, half, rows) + high.astype(f32), 1)
        total = jnp.concatenate(
            [
                part(0, 0, half) + x_low.astype(f32) + y_low.astype(f32),
                part(0, half, rows) + x_top.astype(f32) + y_top.astype(f32),
            ],
            axis=0,
        )
        return total, extra
    live = {k: part(k, 0, rows) for k in range(c_bit)}
    for bit in ctx_bits + [x_bit]:
        low = [k for k in sorted(live) if not k & bit]
        got = send(jnp.stack([live[k ^ bit] for k in low], 0), bit).astype(f32)
        live = {k: live[k] + got[i] for i, k in enumerate(low)}
    return live[0], extra


def slots_to_members(table, index):
    count = table.shape[0]
    bits = count.bit_length() - 1
    grid = table.reshape((2,) * bits + table.shape[1:])
    for b in range(bits):
        taken = (index >> (bits - 1 - b)) & 1
        grid = jnp.where(taken == 1, jnp.flip(grid, b), grid)
    return grid.reshape(table.shape)


def pack_heads(mats, members, heads):
    _, rows8, features = mats.shape
    rows, width = (rows8 - 8, heads * HD)

    def kernel(src_ref, out_ref):
        tail = sum(src_ref[i, rows:, : 3 * width].astype(f32) for i in range(4)).astype(bf16)
        for j in range(members):
            out_ref[j, rows:, :] = tail
            lo, hi = (min(j * width, features), min(j * width + width, features))
            for m in range(3):
                at = m * width
                if hi - lo < width:
                    out_ref[j, :rows, at : at + width] = jnp.zeros((rows, width), bf16)
                if hi > lo:
                    out_ref[j, :rows, at : at + hi - lo] = src_ref[m, :rows, lo:hi]

    return pl.pallas_call(
        kernel,
        out_shape=jax.ShapeDtypeStruct((members, rows8, 3 * width), bf16),
        name="pack_heads",
    )(mats)


def unpack_heads(moved, out_rows, heads):
    members, rows, _ = moved.shape
    features, width = (out_rows.shape[1], heads * HD)

    def kernel(src_ref, last_ref, out_ref):
        out_ref[3] = last_ref[...]
        for j in range(members):
            lo, hi = (min(j * width, features), min(j * width + width, features))
            for m in range(3):
                if hi > lo:
                    out_ref[m, :, lo:hi] = src_ref[j, :, m * width : m * width + hi - lo]

    return pl.pallas_call(
        kernel,
        out_shape=jax.ShapeDtypeStruct((4, rows, features), bf16),
        name="unpack_heads",
    )(moved, out_rows)


def causal_mask(length, shift):
    shape = (length, length)
    row_pos = lax.broadcasted_iota(jnp.int32, shape, 0) ^ shift
    col_pos = lax.broadcasted_iota(jnp.int32, shape, 1) ^ shift
    return row_pos >= col_pos


def split_heads(array, length, heads):
    return array.reshape(-1, length, heads, HD)


def long_scores(qkv, shift, length, heads):
    q, k, v = [split_heads(part, length, heads) for part in jnp.split(qkv, 3, axis=1)]
    scores = jnp.einsum("sthd,slhd->shtl", q, k, preferred_element_type=f32) * score_scale
    return q, k, v, jnp.where(causal_mask(length, shift), scores, masked_fill)


def long_forward(qkv, shift, length, heads):
    total, width3 = qkv.shape
    _, _, v, masked = long_scores(qkv, shift, length, heads)
    log_total = jax.nn.logsumexp(masked, axis=-1, keepdims=True)
    prob = jnp.exp(masked - log_total).astype(bf16)
    ctx = jnp.einsum("shtl,slhd->hdst", prob, v, preferred_element_type=f32)
    return ctx.astype(bf16).reshape(width3 // 3, total), log_total


def long_backward(qkv, grad_ctx, log_total, shift, length, heads):
    q, k, v, masked = long_scores(qkv, shift, length, heads)
    g = split_heads(grad_ctx, length, heads)
    prob = jnp.exp(masked - log_total)
    grad_prob = jnp.einsum("sthd,slhd->shtl", g, v, preferred_element_type=f32)
    delta = jnp.sum(prob * grad_prob, axis=-1, keepdims=True)
    grad_score = (prob * (grad_prob - delta) * score_scale).astype(bf16)
    grads = jnp.concatenate(
        [
            jnp.einsum(spec, left, right, preferred_element_type=f32).reshape(qkv.shape[0], -1)
            for spec, left, right in (
                ("shtl,slhd->sthd", grad_score, k),
                ("shtl,sthd->slhd", grad_score, q),
                ("shtl,sthd->slhd", prob.astype(bf16), g),
            )
        ],
        axis=1,
    )
    return grads.astype(bf16), jnp.sum(grads, axis=0)[None, None]


def attention_forward(qkv, shift, length, heads):
    if length > 256:
        return long_forward(qkv, shift, length, heads)
    total, width3 = qkv.shape
    width = width3 // 3

    def kernel(scal_ref, qkv_ref, ctx_ref, log_ref):
        mask = causal_mask(length, scal_ref[0])
        for h in range(heads):
            lo = h * HD
            q = qkv_ref[:, lo : lo + HD]
            k = qkv_ref[:, width + lo : width + lo + HD]
            v = qkv_ref[:, 2 * width + lo : 2 * width + lo + HD]
            scores = product(q, k, 1, 1) * score_scale
            masked = jnp.where(mask, scores, masked_fill)
            row_max = jnp.max(masked, axis=-1, keepdims=True)
            total_exp = jnp.sum(jnp.exp(masked - row_max), axis=-1, keepdims=True)
            log_total = row_max + jnp.log(total_exp)
            prob = jnp.where(mask, jnp.exp(masked - log_total), 0.0).astype(bf16)
            ctx = product(prob, v, 1, 0)
            ctx_ref[lo : lo + HD, :] = ctx.T.astype(bf16)
            log_ref[:, h : h + 1] = log_total

    return pl.pallas_call(
        kernel,
        out_shape=(
            jax.ShapeDtypeStruct((width, total), bf16),
            jax.ShapeDtypeStruct((total, heads), f32),
        ),
        grid_spec=pltpu.PrefetchScalarGridSpec(
            num_scalar_prefetch=1,
            grid=(total // length,),
            in_specs=[pl.BlockSpec((length, width3), lambda i, s: (i, 0))],
            out_specs=[
                pl.BlockSpec((width, length), lambda i, s: (0, i)),
                pl.BlockSpec((length, heads), lambda i, s: (i, 0)),
            ],
        ),
        name="attention_forward",
    )(shift.reshape(1), qkv)


def attention_backward(qkv, grad_ctx, log_total, shift, length, heads):
    if length > 256:
        return long_backward(qkv, grad_ctx, log_total, shift, length, heads)
    total, width3 = qkv.shape
    width = width3 // 3

    def kernel(scal_ref, qkv_ref, gctx_ref, log_ref, grad_ref, sum_ref):
        mask = causal_mask(length, scal_ref[0])
        for h in range(heads):
            lo = h * HD
            q = qkv_ref[:, lo : lo + HD]
            k = qkv_ref[:, width + lo : width + lo + HD]
            v = qkv_ref[:, 2 * width + lo : 2 * width + lo + HD]
            g = gctx_ref[:, lo : lo + HD]
            scores = product(q, k, 1, 1) * score_scale
            prob = jnp.exp(jnp.where(mask, scores - log_ref[:, h : h + 1], masked_fill))
            grad_prob = product(g, v, 1, 1)
            delta = jnp.sum(prob * grad_prob, axis=-1, keepdims=True)
            grad_score = (prob * (grad_prob - delta) * score_scale).astype(bf16)
            grads = (
                product(grad_score, k, 1, 0),
                product(grad_score, q, 0, 0),
                product(prob.astype(bf16), g, 0, 0),
            )
            for n, grad in enumerate(grads):
                at = n * width + lo
                grad_ref[:, at : at + HD] = grad.astype(bf16)
                col_sum = jnp.sum(grad, axis=0, keepdims=True)
                sum_ref[0, :, at : at + HD] = jnp.broadcast_to(col_sum, (8, HD))

    count = total // length
    return pl.pallas_call(
        kernel,
        out_shape=(
            jax.ShapeDtypeStruct((total, width3), bf16),
            jax.ShapeDtypeStruct((count, 8, width3), f32),
        ),
        grid_spec=pltpu.PrefetchScalarGridSpec(
            num_scalar_prefetch=1,
            grid=(count,),
            in_specs=[
                pl.BlockSpec((length, width3), lambda i, s: (i, 0)),
                pl.BlockSpec((length, width), lambda i, s: (i, 0)),
                pl.BlockSpec((length, heads), lambda i, s: (i, 0)),
            ],
            out_specs=[
                pl.BlockSpec((length, width3), lambda i, s: (i, 0)),
                pl.BlockSpec((1, 8, width3), lambda i, s: (i, 0, 0)),
            ],
        ),
        name="attention_backward",
    )(shift.reshape(1), qkv, grad_ctx, log_total)


def body(
    tokens,
    attn_weight,
    up_weight,
    down_weight,
    vectors,
    attn_moments,
    up_moments,
    down_moments,
    vector_moments,
    cotangent,
):
    seq_count, rows, features = tokens.shape
    nz = lax.axis_size("z")
    n_ctx = lax.axis_size("ctx")
    members = 4 * n_ctx
    nzz = nz // 4
    g = lax.axis_index(PLANE).astype(jnp.int32)
    shift = (lax.axis_index("ctx") * rows).astype(jnp.int32)
    length = n_ctx * rows
    heads = -(-H // members)
    width = heads * HD
    padded = members * width
    attn_piece = attn_weight.shape[0]
    unit_piece = down_weight.shape[0]
    vec_piece = vectors.shape[0]
    own_tokens = tokens.reshape(rows, features)
    own_cot = cotangent.reshape(rows, features)

    z = lax.axis_index("z").astype(jnp.int32)
    vec_rows = jnp.zeros((8, features), bf16)
    vec_rows = lax.dynamic_update_slice(vec_rows, vectors.astype(bf16)[None], (z, 0))
    attn_packed = jnp.concatenate([attn_weight.astype(bf16), vec_rows], 0)
    attn_z = lax.all_gather(attn_packed, "z", axis=0, tiled=False)
    tokens_x = plane_gather(own_tokens).reshape(members * rows, features)
    cot_x = plane_gather(own_cot).reshape(members * rows, features)
    mlp_packed = jnp.concatenate([up_weight.astype(bf16).T, down_weight.astype(bf16)], 0)
    mlp_z = lax.all_gather(mlp_packed, "z", axis=0, tiled=False)
    up_mine = mlp_z[:, :unit_piece].reshape(nz * unit_piece, features)
    down_mine = mlp_z[:, unit_piece:].reshape(nz * unit_piece, features)

    attn_mats = attn_z[:, :attn_piece].reshape(4, nzz * attn_piece, features)
    if nzz == 1:
        qkv_rows = pack_heads(attn_z, members, heads)
    else:
        qkv_rows = jnp.pad(attn_mats[:3], ((0, 0), (0, 0), (0, padded - features)))
        qkv_rows = qkv_rows.reshape(3, nzz * attn_piece, members, width).transpose(2, 1, 0, 3)
        qkv_rows = qkv_rows.reshape(members, nzz * attn_piece, 3 * width)
        tail = jnp.sum(attn_z[:, attn_piece:, : 3 * width].astype(f32), axis=0).astype(bf16)
        tail = jnp.broadcast_to(tail, (members,) + tail.shape)
        qkv_rows = jnp.concatenate([qkv_rows, tail], axis=1)
    w_moved = lax.all_to_all(qkv_rows, PLANE, 0, 0, tiled=True)
    w_qkv = w_moved[:, : nzz * attn_piece]
    w_qkv = w_qkv.reshape(members, nzz, attn_piece, 3 * width).transpose(1, 0, 2, 3)
    w_qkv = w_qkv.reshape(features, 3 * width)
    w_out = plane_gather(attn_mats[3], g)
    w_out = w_out.reshape(members, nzz, attn_piece, features).transpose(1, 0, 2, 3)
    w_out = w_out.reshape(features, features)

    vec_all = w_moved[:, nzz * attn_piece :][:, :nz, :vec_piece].astype(f32)
    table = vec_all.transpose(1, 0, 2).reshape(features, 12).T
    gain_one, bias_one, gain_two, bias_two, bias_query, bias_value, bias_out, bias_down = [
        table[i] for i in range(8)
    ]
    bias_up = table[8:].T.reshape(nz, members, unit_piece)
    bias_up = lax.dynamic_slice_in_dim(bias_up, g, 1, 1).reshape(nz * unit_piece)

    def head_slice(vec):
        return lax.dynamic_slice_in_dim(jnp.pad(vec, (0, padded - features)), g * width, width)

    token_f = tokens_x.astype(f32)
    norm_one = layer_norm_forward(token_f, gain_one, bias_one)[0].astype(bf16)
    bias_qkv = jnp.concatenate(
        [head_slice(bias_query), jnp.zeros((width,), f32), head_slice(bias_value)]
    )
    qkv = (product(norm_one, w_qkv, 1, 0) + bias_qkv).astype(bf16)
    ctx_mine, log_total = attention_forward(qkv, shift, length, heads)
    ctx_all = plane_gather(ctx_mine, g, rows)
    ctx_all = ctx_all.reshape(padded, members * rows)[:features]

    resid_mid = token_f + product(ctx_all, w_out, 0, 0) + bias_out
    norm_two = layer_norm_forward(resid_mid, gain_two, bias_two)[0].astype(bf16)
    pre_act = product(norm_two, up_mine, 1, 1) + bias_up
    activated, act_slope = gelu_pair(pre_act)
    hidden_b = activated.astype(bf16)
    grad_pre = product(cot_x, down_mine, 1, 1) * act_slope
    grad_pre_b = grad_pre.astype(bf16)

    def owner_send(blocks):
        return [
            lax.ppermute(
                lax.dynamic_index_in_dim(blocks, (z + d) % nz, 0, False),
                "z",
                [(i, (i + d) % nz) for i in range(nz)],
            )
            for d in range(1, nz)
        ]

    def owner_total(blocks, received):
        total = lax.dynamic_index_in_dim(blocks, z, 0, False).astype(f32)
        for piece in received:
            total = total + piece.astype(f32)
        return total


    def mlp_products():
        up_local = product(grad_pre_b, norm_two, 0, 0).reshape(nz, unit_piece, features)
        down_local = product(hidden_b, cot_x, 0, 0).reshape(nz, unit_piece, features)
        return jnp.concatenate([up_local.astype(bf16), down_local.astype(bf16)], 1)

    grad_second, mlp_local = plane_sum(grad_pre_b, up_mine, 0, mlp_products)
    with jax.named_scope("unit_exchange"):
        mlp_got = owner_send(mlp_local)
    own_mid = resid_mid[:rows]
    _, xhat_two, rstd_two = layer_norm_forward(own_mid, gain_two, bias_two)
    cot_f = own_cot.astype(f32)
    grad_resid = cot_f + layer_norm_backward(grad_second, gain_two, xhat_two, rstd_two)
    grad_resid_x = plane_gather(grad_resid.astype(bf16)).reshape(members * rows, features)

    w_out_heads = lax.dynamic_slice_in_dim(
        jnp.pad(w_out, ((0, padded - features), (0, 0))), g * width, width, 0
    )
    grad_ctx = product(grad_resid_x, w_out_heads, 1, 1).astype(bf16)
    with jax.named_scope("attend_back"):
        grad_qkv, qkv_sums = attention_backward(qkv, grad_ctx, log_total, shift, length, heads)
    qkv_local = product(norm_one, grad_qkv, 0, 0).astype(bf16)
    qkv_local = qkv_local.reshape(nzz, members, attn_piece, 3 * width).transpose(1, 0, 2, 3)
    qkv_local = qkv_local.reshape(members, nzz * attn_piece, 3 * width)
    qkv_moved = lax.all_to_all(qkv_local, PLANE, 0, 0, tiled=True)
    ctx_rows = ctx_all.reshape(nzz, members, attn_piece, members * rows)
    ctx_rows = lax.dynamic_slice_in_dim(ctx_rows, g, 1, 1)
    ctx_rows = ctx_rows.reshape(nzz * attn_piece, members * rows)
    out_local = product(ctx_rows, grad_resid_x, 1, 0).astype(bf16)
    grad_first, _ = plane_sum(grad_qkv, w_qkv, 1)
    _, xhat_one, rstd_one = layer_norm_forward(own_tokens.astype(f32), gain_one, bias_one)
    block_input_gradient = grad_resid + layer_norm_backward(
        grad_first, gain_one, xhat_one, rstd_one
    )

    if nzz == 1:
        attn_local = unpack_heads(qkv_moved, out_local, heads)
    else:
        qkv_moved = qkv_moved.reshape(members, nzz * attn_piece, 3, width).transpose(2, 1, 0, 3)
        qkv_moved = qkv_moved.reshape(3, nzz * attn_piece, padded)[:, :, :features]
        attn_local = jnp.concatenate([qkv_moved, out_local[None]], 0)
    attn_local = attn_local.reshape(nz, attn_piece, features)
    attn_grad = owner_total(attn_local, owner_send(attn_local))
    mlp_sum = owner_total(mlp_local, mlp_got)
    up_grad = mlp_sum[:unit_piece].T
    down_grad = mlp_sum[unit_piece:]

    held, _ = lax.optimization_barrier((hidden_b, qkv_moved))
    block_out = own_mid + plane_sum(held, down_mine, 0)[0] + bias_down

    qkv_total = jnp.sum(qkv_sums[:, 0], axis=0)

    def place_heads(vec):
        return lax.dynamic_update_slice(jnp.zeros((padded,), f32), vec, (g * width,))[:features]

    unit_sums = jnp.sum(grad_pre, axis=0).reshape(nz, 1, unit_piece)
    unit_sums = lax.dynamic_update_slice(
        jnp.zeros((nz, members, unit_piece), f32), unit_sums, (0, g, 0)
    ).reshape(features, 4)
    vector_rows = jnp.stack(
        [
            jnp.sum(grad_first * xhat_one, axis=0),
            jnp.sum(grad_first, axis=0),
            jnp.sum(grad_second * xhat_two, axis=0),
            jnp.sum(grad_second, axis=0),
            place_heads(qkv_total[:width]),
            place_heads(qkv_total[2 * width :]),
            jnp.sum(grad_resid, axis=0),
            jnp.sum(cot_f, axis=0),
        ],
        0,
    )
    vector_local = jnp.concatenate([vector_rows.T, unit_sums], axis=1)
    vector_local, _ = lax.optimization_barrier((vector_local, qkv_moved))
    vector_moved = lax.all_to_all(
        vector_local.reshape(nz * members, vec_piece), ("z",) + PLANE, 0, 0, tiled=True
    )
    vector_grad = jnp.sum(vector_moved, axis=0)

    attn_new, attn_moments_new = adam_update(attn_weight, attn_moments, attn_grad, decay_rate)
    up_new, up_moments_new = adam_update(up_weight, up_moments, up_grad, decay_rate)
    down_new, down_moments_new = adam_update(down_weight, down_moments, down_grad, decay_rate)
    vector_new, vector_moments_new = adam_update(vectors, vector_moments, vector_grad, 0.0)
    return (
        block_out.reshape(seq_count, rows, features),
        block_input_gradient.reshape(seq_count, rows, features),
        attn_grad,
        up_grad,
        down_grad,
        vector_grad,
        attn_new,
        up_new,
        down_new,
        vector_new,
        attn_moments_new,
        up_moments_new,
        down_moments_new,
        vector_moments_new,
    )


def solution(mesh):
    n_data, n_ctx = mesh.shape["dp"], mesh.shape["ctx"]
    fine = Mesh(mesh.devices.reshape(n_data // 4, 2, 2, n_ctx), ("z", "x", "c", "ctx"))
    data = ("z", "x", "c")
    every = ("z", "x", "c", "ctx")
    rows_spec = P(data, "ctx", None)
    in_specs = (
        rows_spec,
        P(every, None),
        P(None, every),
        P(every, None),
        P(every),
        P(None, every, None),
        P(None, None, every),
        P(None, every, None),
        P(None, every),
        rows_spec,
    )
    out_specs = (
        rows_spec,
        rows_spec,
        P(every, None),
        P(None, every),
        P(every, None),
        P(every),
        P(every, None),
        P(None, every),
        P(every, None),
        P(every),
        P(None, every, None),
        P(None, None, every),
        P(None, every, None),
        P(None, every),
    )
    return jax.shard_map(body, mesh=fine, in_specs=in_specs, out_specs=out_specs, check_vma=False)
```

```python
import jax
import jax.numpy as jnp
from jax import lax
from jax.experimental import pallas as pl
from jax.experimental.pallas import tpu as pltpu
from jax.sharding import Mesh, PartitionSpec as P


H = 17
HD = 64
PLANE = ("x", "c", "ctx")

norm_eps = 1e-05
beta_one = 0.9
beta_two = 0.95
adam_eps = 1e-08
learn_rate = 0.06
decay_rate = 0.1
first_fix = 1.0 - 0.9**5.0
second_fix = 1.0 - 0.95**5.0
masked_fill = -1e30
score_scale = HD ** (-0.5)
bf16 = jnp.bfloat16
f32 = jnp.float32


def gelu_pair(pre_act):
    cumulative = 0.5 * (1.0 + lax.erf(pre_act * 0.7071067811865476))
    density = jnp.exp(-0.5 * pre_act * pre_act) * 0.3989422804014327
    return (pre_act * cumulative, cumulative + pre_act * density)


def layer_norm_forward(resid, gain_vec, offset):
    center = resid - jnp.mean(resid, axis=-1, keepdims=True)
    inv_std = lax.rsqrt(jnp.mean(center * center, axis=-1, keepdims=True) + norm_eps)
    normed = center * inv_std
    return (normed * gain_vec + offset, normed, inv_std)


def layer_norm_backward(grad_norm, gain_vec, normed, inv_std):
    scaled = grad_norm * gain_vec
    return inv_std * (
        scaled
        - jnp.mean(scaled, axis=-1, keepdims=True)
        - normed * jnp.mean(scaled * normed, axis=-1, keepdims=True)
    )


def product(left, right, left_dim, right_dim):
    return lax.dot_general(
        left, right, (((left_dim,), (right_dim,)), ((), ())), preferred_element_type=f32
    )


def adam_update(weight, moments, gradient, decay_factor):
    mean_new = beta_one * moments[0] + (1.0 - beta_one) * gradient
    square_new = beta_two * moments[1] + (1.0 - beta_two) * gradient * gradient
    update_dir = mean_new / first_fix / (jnp.sqrt(square_new / second_fix) + adam_eps)
    return (
        weight - learn_rate * (update_dir + decay_factor * weight),
        jnp.stack([mean_new, square_new], 0),
    )


def plane_bits():
    n_ctx = lax.axis_size("ctx")
    ctx_bits = [1 << b for b in range(n_ctx.bit_length() - 1)]
    return n_ctx, 2 * n_ctx, ctx_bits


def member_bits(slot):
    x_bit, c_bit, _ = plane_bits()
    low = slot % x_bit
    return low + (c_bit if slot & x_bit else 0) + (x_bit if slot & c_bit else 0)


def swap(piece, bit):
    members = 4 * lax.axis_size("ctx")
    return lax.ppermute(piece, PLANE, [(i, i ^ member_bits(bit)) for i in range(members)])


def assemble(parts, shape, index=None, lane_block=0):
    scal = jnp.zeros((1,), jnp.int32) if index is None else index.reshape(1)

    def kernel(scal_ref, *refs):
        out_ref = refs[len(parts)]
        for (slot, row, array), ref in zip(parts, refs):
            place = slot if index is None else scal_ref[0] ^ member_bits(slot)
            last = row + array.shape[0]
            if not lane_block:
                out_ref[place, row:last, :] = ref[...]
                continue
            for t in range(shape[0]):
                s = t ^ slot
                out_ref[place, row:last, t * lane_block : (t + 1) * lane_block] = ref[
                    :, s * lane_block : (s + 1) * lane_block
                ]

    def whole(array_shape):
        return pl.BlockSpec(array_shape, lambda i, s: (0,) * len(array_shape))

    return pl.pallas_call(
        kernel,
        out_shape=jax.ShapeDtypeStruct(shape, parts[0][2].dtype),
        grid_spec=pltpu.PrefetchScalarGridSpec(
            num_scalar_prefetch=1,
            grid=(1,),
            in_specs=[whole(array.shape) for _, _, array in parts],
            out_specs=whole(shape),
        ),
        name="assemble",
    )(scal, *[array for _, _, array in parts])


def plane_gather(piece, index=None, lane_block=0):
    x_bit, c_bit, ctx_bits = plane_bits()
    half = piece.shape[0] // 16 * 8
    shape = (4 * lax.axis_size("ctx"),) + piece.shape
    if len(ctx_bits) == 1:
        from_x, from_y, from_c = (swap(piece, x_bit), swap(piece, 1), swap(piece, c_bit))
        diag_low = swap(from_x[:half], 1)
        diag_high = swap(from_y[half:], x_bit)
        cx, cy = (swap(from_x, c_bit), swap(from_y, c_bit))
        c_low, c_high = (swap(diag_low, c_bit), swap(diag_high, c_bit))
        xy, xc, yc, xyc = (x_bit + 1, x_bit + c_bit, c_bit + 1, x_bit + c_bit + 1)
        parts = [(0, 0, piece), (1, 0, from_y), (c_bit, 0, from_c), (yc, 0, cy)]
        parts += [(x_bit, 0, from_x), (xy, 0, diag_low), (xy, half, diag_high), (xc, 0, cx)]
        parts += [(xyc, 0, c_low), (xyc, half, c_high)]
        return assemble(parts, shape, index, lane_block)
    offsets, whole = [0], piece[None]
    for bit in [x_bit] + ctx_bits + [c_bit]:
        whole = jnp.concatenate([whole, swap(whole, bit)], axis=0)
        offsets = offsets + [o ^ bit for o in offsets]
    order = [offsets.index(k) for k in range(len(offsets))]
    whole = jnp.concatenate([whole[o : o + 1] for o in order], axis=0)
    if lane_block:
        whole = jnp.stack(
            [
                whole[k].reshape(piece.shape[0], -1, lane_block)[:, [t ^ k for t in range(shape[0])]]
                for k in range(shape[0])
            ]
        ).reshape(shape)
    if index is None:
        return whole
    swapped = jnp.stack([whole[member_bits(k)] for k in range(shape[0])])
    return slots_to_members(swapped, index)


def lane_padded(features):
    return -(-features // 128) * 128


def store_padded(ref, value):
    width = value.shape[1]
    ref[:, :width] = value
    if ref.shape[1] > width:
        ref[:, width:] = jnp.zeros((value.shape[0], ref.shape[1] - width), value.dtype)


def split_sum(kept, moved, rows):
    half, width = (rows // 2, kept.shape[1])
    wire, total = (jax.ShapeDtypeStruct((half, width), d) for d in (bf16, f32))

    def kernel(kept_ref, moved_ref, low, high, x_top, y_low, x_low, y_top, mine):
        def part(slot, second):
            at = slice(slot * rows + second * half, slot * rows + second * half + half)
            return kept_ref[at] + moved_ref[at, :width].astype(f32)

        low[...] = part(3, 0).astype(bf16)
        high[...] = part(3, 1).astype(bf16)
        x_top[...] = part(2, 1).astype(bf16)
        y_low[...] = part(1, 0).astype(bf16)
        x_low[...] = part(2, 0)
        y_top[...] = part(1, 1)
        mine[:half] = part(0, 0)
        mine[half:] = part(0, 1)

    return pl.pallas_call(
        kernel,
        out_shape=(wire, wire, wire, wire, total, total)
        + (jax.ShapeDtypeStruct((rows, width), f32),),
        name="split_sum",
    )(kept, moved)


def plane_sum(kept, moved):
    x_bit, c_bit, ctx_bits = plane_bits()
    rows = kept.shape[0] // c_bit
    if len(ctx_bits) == 1:
        low, high, x_top, y_low, x_low, y_top, mine = split_sum(kept, moved, rows)
        low, high = (swap(low, 1), swap(high, x_bit))
        x_top, y_low = (swap(x_top, x_bit), swap(y_low, 1))
        x_low = swap((x_low + low.astype(f32)).astype(bf16), x_bit)
        y_top = swap((y_top + high.astype(f32)).astype(bf16), 1)
        half = rows // 2
        first = mine[:half] + x_low.astype(f32) + y_low.astype(f32)
        second = mine[half:] + x_top.astype(f32) + y_top.astype(f32)
        return jnp.concatenate([first, second], axis=0)
    live = kept + moved[:, : kept.shape[1]].astype(f32)
    live = {k: live[k * rows : (k + 1) * rows] for k in range(c_bit)}
    for bit in ctx_bits + [x_bit]:
        low = [k for k in sorted(live) if not k & bit]
        got = swap(jnp.stack([live[k ^ bit] for k in low], 0).astype(bf16), bit).astype(f32)
        live = {k: live[k] + got[i] for i, k in enumerate(low)}
    return live[0]


def unit_pass(ctx_all, w_out, tokens_x, cot_x, up_mine, down_mine, vecs, bias_up, rows):
    total, features = tokens_x.shape
    units = up_mine.shape[0]
    block = min(256, total // 2)
    steps = total // block
    near = steps // 2

    def kernel(
        ctx_ref, w_ref, tok_ref, cot_ref, up_ref, down_ref, vec_ref, bias_ref,
        norm_ref, hid_ref, pre_ref, sec_far, sec_near, out_far, out_near, mid_ref, sum_ref,
    ):
        step = pl.program_id(0)
        resid = tok_ref[...].astype(f32) + product(ctx_ref[:features], w_ref[...], 0, 0)
        resid = resid + vec_ref[2:3]
        norm_two = layer_norm_forward(resid, vec_ref[0:1], vec_ref[1:2])[0].astype(bf16)
        norm_ref[...] = norm_two
        pre_act = product(norm_two, up_ref[...], 1, 1) + bias_ref[...]
        activated, slope = gelu_pair(pre_act)
        hidden = activated.astype(bf16)
        grad_pre = product(cot_ref[...], down_ref[...], 1, 1) * slope
        grad_pre_b = grad_pre.astype(bf16)
        hid_ref[...] = hidden
        pre_ref[...] = grad_pre_b
        second = product(grad_pre_b, up_ref[...], 1, 0)
        out = product(hidden, down_ref[...], 1, 0)
        sums = jnp.broadcast_to(jnp.sum(grad_pre, axis=0, keepdims=True), (8, units))

        @pl.when(step == 0)
        def _():
            sum_ref[...] = sums

        @pl.when(step > 0)
        def _():
            sum_ref[...] += sums

        @pl.when(step < near)
        def _():
            store_padded(sec_far, second.astype(bf16))
            store_padded(out_far, out.astype(bf16))

        @pl.when(step >= near)
        def _():
            sec_near[...] = second
            out_near[...] = out

        @pl.when(step == near)
        def _():
            mid_ref[...] = resid[:rows]

    def here(i):
        return (i + near) % steps

    def whole(array):
        return pl.BlockSpec(array.shape, lambda i: (0, 0))

    by_rows = pl.BlockSpec((block, features), lambda i: (here(i), 0))
    by_units = pl.BlockSpec((block, units), lambda i: (here(i), 0))
    wide = lane_padded(features)
    far = pl.BlockSpec((block, wide), lambda i: (jnp.minimum(i, near - 1), 0))
    close = pl.BlockSpec((block, features), lambda i: (jnp.maximum(i - near, 0), 0))
    shape = jax.ShapeDtypeStruct
    return pl.pallas_call(
        kernel,
        grid=(steps,),
        out_shape=(
            shape((total, features), bf16),
            shape((total, units), bf16),
            shape((total, units), bf16),
            shape((total // 2, wide), bf16),
            shape((total // 2, features), f32),
            shape((total // 2, wide), bf16),
            shape((total // 2, features), f32),
            shape((rows, features), f32),
            shape((8, units), f32),
        ),
        in_specs=[
            pl.BlockSpec((ctx_all.shape[0], block), lambda i: (0, here(i))),
            whole(w_out), by_rows, by_rows, whole(up_mine), whole(down_mine),
            whole(vecs), whole(bias_up),
        ],
        out_specs=(
            by_rows, by_units, by_units, far, close, far, close,
            pl.BlockSpec((rows, features), lambda i: (0, 0)),
            pl.BlockSpec((8, units), lambda i: (0, 0)),
        ),
        name="unit_pass",
    )(ctx_all, w_out, tokens_x, cot_x, up_mine, down_mine, vecs, bias_up)


def slots_to_members(table, index):
    count = table.shape[0]
    bits = count.bit_length() - 1
    grid = table.reshape((2,) * bits + table.shape[1:])
    for b in range(bits):
        taken = (index >> (bits - 1 - b)) & 1
        grid = jnp.where(taken == 1, jnp.flip(grid, b), grid)
    return grid.reshape(table.shape)


def pack_heads(mats, members, heads):
    _, rows8, features = mats.shape
    rows, width = (rows8 - 8, heads * HD)

    def kernel(src_ref, out_ref):
        tail = sum(src_ref[i, rows:, : 3 * width].astype(f32) for i in range(4)).astype(bf16)
        for j in range(members):
            out_ref[j, rows:, :] = tail
            lo, hi = (min(j * width, features), min(j * width + width, features))
            for m in range(3):
                at = m * width
                if hi - lo < width:
                    out_ref[j, :rows, at : at + width] = jnp.zeros((rows, width), bf16)
                if hi > lo:
                    out_ref[j, :rows, at : at + hi - lo] = src_ref[m, :rows, lo:hi]

    return pl.pallas_call(
        kernel,
        out_shape=jax.ShapeDtypeStruct((members, rows8, 3 * width), bf16),
        name="pack_heads",
    )(mats)


def unpack_heads(moved, out_rows, heads):
    members, rows, _ = moved.shape
    features, width = (out_rows.shape[1], heads * HD)

    def kernel(src_ref, last_ref, out_ref):
        out_ref[3] = last_ref[...]
        for j in range(members):
            lo, hi = (min(j * width, features), min(j * width + width, features))
            for m in range(3):
                if hi > lo:
                    out_ref[m, :, lo:hi] = src_ref[j, :, m * width : m * width + hi - lo]

    return pl.pallas_call(
        kernel,
        out_shape=jax.ShapeDtypeStruct((4, rows, features), bf16),
        name="unpack_heads",
    )(moved, out_rows)


def causal_mask(length, shift):
    shape = (length, length)
    row_pos = lax.broadcasted_iota(jnp.int32, shape, 0) ^ shift
    col_pos = lax.broadcasted_iota(jnp.int32, shape, 1) ^ shift
    return row_pos >= col_pos


def split_heads(array, length, heads):
    return array.reshape(-1, length, heads, HD)


def long_scores(qkv, shift, length, heads):
    q, k, v = [split_heads(part, length, heads) for part in jnp.split(qkv, 3, axis=1)]
    scores = jnp.einsum("sthd,slhd->shtl", q, k, preferred_element_type=f32) * score_scale
    return q, k, v, jnp.where(causal_mask(length, shift), scores, masked_fill)


def long_forward(qkv, shift, length, heads):
    total, width3 = qkv.shape
    _, _, v, masked = long_scores(qkv, shift, length, heads)
    log_total = jax.nn.logsumexp(masked, axis=-1, keepdims=True)
    prob = jnp.exp(masked - log_total).astype(bf16)
    ctx = jnp.einsum("shtl,slhd->hdst", prob, v, preferred_element_type=f32)
    return ctx.astype(bf16).reshape(width3 // 3, total), log_total


def long_backward(qkv, grad_ctx, log_total, shift, length, heads):
    q, k, v, masked = long_scores(qkv, shift, length, heads)
    g = split_heads(grad_ctx, length, heads)
    prob = jnp.exp(masked - log_total)
    grad_prob = jnp.einsum("sthd,slhd->shtl", g, v, preferred_element_type=f32)
    delta = jnp.sum(prob * grad_prob, axis=-1, keepdims=True)
    grad_score = (prob * (grad_prob - delta) * score_scale).astype(bf16)
    grads = jnp.concatenate(
        [
            jnp.einsum(spec, left, right, preferred_element_type=f32).reshape(qkv.shape[0], -1)
            for spec, left, right in (
                ("shtl,slhd->sthd", grad_score, k),
                ("shtl,sthd->slhd", grad_score, q),
                ("shtl,sthd->slhd", prob.astype(bf16), g),
            )
        ],
        axis=1,
    )
    return grads.astype(bf16), jnp.sum(grads, axis=0)[None, None]


def attention_forward(qkv, shift, length, heads):
    if length > 256:
        return long_forward(qkv, shift, length, heads)
    total, width3 = qkv.shape
    width = width3 // 3

    def kernel(scal_ref, qkv_ref, ctx_ref, log_ref):
        mask = causal_mask(length, scal_ref[0])
        for h in range(heads):
            lo = h * HD
            q = qkv_ref[:, lo : lo + HD]
            k = qkv_ref[:, width + lo : width + lo + HD]
            v = qkv_ref[:, 2 * width + lo : 2 * width + lo + HD]
            scores = product(q, k, 1, 1) * score_scale
            masked = jnp.where(mask, scores, masked_fill)
            row_max = jnp.max(masked, axis=-1, keepdims=True)
            total_exp = jnp.sum(jnp.exp(masked - row_max), axis=-1, keepdims=True)
            log_total = row_max + jnp.log(total_exp)
            prob = jnp.where(mask, jnp.exp(masked - log_total), 0.0).astype(bf16)
            ctx = product(prob, v, 1, 0)
            ctx_ref[lo : lo + HD, :] = ctx.T.astype(bf16)
            log_ref[:, h : h + 1] = log_total

    return pl.pallas_call(
        kernel,
        out_shape=(
            jax.ShapeDtypeStruct((width, total), bf16),
            jax.ShapeDtypeStruct((total, heads), f32),
        ),
        grid_spec=pltpu.PrefetchScalarGridSpec(
            num_scalar_prefetch=1,
            grid=(total // length,),
            in_specs=[pl.BlockSpec((length, width3), lambda i, s: (i, 0))],
            out_specs=[
                pl.BlockSpec((width, length), lambda i, s: (0, i)),
                pl.BlockSpec((length, heads), lambda i, s: (i, 0)),
            ],
        ),
        name="attention_forward",
    )(shift.reshape(1), qkv)


def attention_backward(qkv, grad_x, norm_one, w_heads, w_qkv, log_total, shift, length, heads):
    total, width3 = qkv.shape
    if length > 256:
        grad_ctx = product(grad_x, w_heads, 1, 1).astype(bf16)
        grad_qkv, sums = long_backward(qkv, grad_ctx, log_total, shift, length, heads)
        far = product(grad_qkv[total // 2 :], w_qkv, 1, 1).astype(bf16)
        close = product(grad_qkv[: total // 2], w_qkv, 1, 1)
        return far, close, product(norm_one, grad_qkv, 0, 0).astype(bf16), sums
    width = width3 // 3
    features = norm_one.shape[1]
    wide = lane_padded(features)
    steps = total // length
    near = steps // 2

    def kernel(
        scal_ref, qkv_ref, gx_ref, norm_ref, wh_ref, wq_ref, log_ref,
        far_ref, near_ref, local_ref, sum_ref, grad_ref, acc_ref,
    ):
        step = pl.program_id(0)
        mask = causal_mask(length, scal_ref[0])
        grad_ctx = product(gx_ref[...], wh_ref[...], 1, 1).astype(bf16)
        for h in range(heads):
            lo = h * HD
            q = qkv_ref[:, lo : lo + HD]
            k = qkv_ref[:, width + lo : width + lo + HD]
            v = qkv_ref[:, 2 * width + lo : 2 * width + lo + HD]
            g = grad_ctx[:, lo : lo + HD]
            scores = product(q, k, 1, 1) * score_scale
            prob = jnp.exp(jnp.where(mask, scores - log_ref[:, h : h + 1], masked_fill))
            grad_prob = product(g, v, 1, 1)
            delta = jnp.sum(prob * grad_prob, axis=-1, keepdims=True)
            grad_score = (prob * (grad_prob - delta) * score_scale).astype(bf16)
            grads = (
                product(grad_score, k, 1, 0),
                product(grad_score, q, 0, 0),
                product(prob.astype(bf16), g, 0, 0),
            )
            for n, grad in enumerate(grads):
                at = n * width + lo
                grad_ref[:, at : at + HD] = grad.astype(bf16)
                col_sum = jnp.sum(grad, axis=0, keepdims=True)
                sum_ref[0, :, at : at + HD] = jnp.broadcast_to(col_sum, (8, HD))
        grad_all = grad_ref[...]
        first = product(grad_all, wq_ref[...], 1, 1)
        local = product(norm_ref[...], grad_all, 0, 0)

        @pl.when(step == 0)
        def _():
            acc_ref[...] = local

        @pl.when(step > 0)
        def _():
            acc_ref[...] += local

        @pl.when(step == steps - 1)
        def _():
            local_ref[...] = acc_ref[...].astype(bf16)

        @pl.when(step < near)
        def _():
            store_padded(far_ref, first.astype(bf16))

        @pl.when(step >= near)
        def _():
            near_ref[...] = first

    def by_rows(size):
        return pl.BlockSpec((length, size), lambda i, s: ((i + near) % steps, 0))

    def whole(shape):
        return pl.BlockSpec(shape, lambda i, s: (0, 0))

    return pl.pallas_call(
        kernel,
        out_shape=(
            jax.ShapeDtypeStruct((total // 2, wide), bf16),
            jax.ShapeDtypeStruct((total // 2, features), f32),
            jax.ShapeDtypeStruct((features, width3), bf16),
            jax.ShapeDtypeStruct((steps, 8, width3), f32),
        ),
        grid_spec=pltpu.PrefetchScalarGridSpec(
            num_scalar_prefetch=1,
            grid=(steps,),
            in_specs=[
                by_rows(width3), by_rows(features), by_rows(features),
                whole(w_heads.shape), whole(w_qkv.shape), by_rows(heads),
            ],
            out_specs=[
                pl.BlockSpec((length, wide), lambda i, s: (jnp.minimum(i, near - 1), 0)),
                pl.BlockSpec((length, features), lambda i, s: (jnp.maximum(i - near, 0), 0)),
                whole((features, width3)),
                pl.BlockSpec((1, 8, width3), lambda i, s: ((i + near) % steps, 0, 0)),
            ],
            scratch_shapes=[
                pltpu.VMEM((length, width3), bf16),
                pltpu.VMEM((features, width3), f32),
            ],
        ),
        name="attention_backward",
    )(shift.reshape(1), qkv, grad_x, norm_one, w_heads, w_qkv, log_total)


def body(
    tokens,
    attn_weight,
    up_weight,
    down_weight,
    vectors,
    attn_moments,
    up_moments,
    down_moments,
    vector_moments,
    cotangent,
):
    seq_count, rows, features = tokens.shape
    nz = lax.axis_size("z")
    n_ctx = lax.axis_size("ctx")
    members = 4 * n_ctx
    nzz = nz // 4
    g = lax.axis_index(PLANE).astype(jnp.int32)
    shift = (lax.axis_index("ctx") * rows).astype(jnp.int32)
    length = n_ctx * rows
    heads = -(-H // members)
    width = heads * HD
    padded = members * width
    attn_piece = attn_weight.shape[0]
    unit_piece = down_weight.shape[0]
    vec_piece = vectors.shape[0]
    own_tokens = tokens.reshape(rows, features)
    own_cot = cotangent.reshape(rows, features)

    z = lax.axis_index("z").astype(jnp.int32)
    vec_rows = jnp.zeros((8, features), bf16)
    vec_rows = lax.dynamic_update_slice(vec_rows, vectors.astype(bf16)[None], (z, 0))
    attn_packed = jnp.concatenate([attn_weight.astype(bf16), vec_rows], 0)
    attn_z = lax.all_gather(attn_packed, "z", axis=0, tiled=False)
    tokens_x = plane_gather(own_tokens).reshape(members * rows, features)
    cot_x = plane_gather(own_cot).reshape(members * rows, features)
    mlp_packed = jnp.concatenate([up_weight.astype(bf16).T, down_weight.astype(bf16)], 0)
    mlp_z = lax.all_gather(mlp_packed, "z", axis=0, tiled=False)
    up_mine = mlp_z[:, :unit_piece].reshape(nz * unit_piece, features)
    down_mine = mlp_z[:, unit_piece:].reshape(nz * unit_piece, features)

    attn_mats = attn_z[:, :attn_piece].reshape(4, nzz * attn_piece, features)
    if nzz == 1:
        qkv_rows = pack_heads(attn_z, members, heads)
    else:
        qkv_rows = jnp.pad(attn_mats[:3], ((0, 0), (0, 0), (0, padded - features)))
        qkv_rows = qkv_rows.reshape(3, nzz * attn_piece, members, width).transpose(2, 1, 0, 3)
        qkv_rows = qkv_rows.reshape(members, nzz * attn_piece, 3 * width)
        tail = jnp.sum(attn_z[:, attn_piece:, : 3 * width].astype(f32), axis=0).astype(bf16)
        tail = jnp.broadcast_to(tail, (members,) + tail.shape)
        qkv_rows = jnp.concatenate([qkv_rows, tail], axis=1)
    w_moved = lax.all_to_all(qkv_rows, PLANE, 0, 0, tiled=True)
    w_qkv = w_moved[:, : nzz * attn_piece]
    w_qkv = w_qkv.reshape(members, nzz, attn_piece, 3 * width).transpose(1, 0, 2, 3)
    w_qkv = w_qkv.reshape(features, 3 * width)
    w_out = plane_gather(attn_mats[3], g)
    w_out = w_out.reshape(members, nzz, attn_piece, features).transpose(1, 0, 2, 3)
    w_out = w_out.reshape(features, features)

    vec_all = w_moved[:, nzz * attn_piece :][:, :nz, :vec_piece].astype(f32)
    table = vec_all.transpose(1, 0, 2).reshape(features, 12).T
    gain_one, bias_one, gain_two, bias_two, bias_query, bias_value, bias_out, bias_down = [
        table[i] for i in range(8)
    ]
    bias_up = table[8:].T.reshape(nz, members, unit_piece)
    bias_up = lax.dynamic_slice_in_dim(bias_up, g, 1, 1).reshape(nz * unit_piece)

    def head_slice(vec):
        return lax.dynamic_slice_in_dim(jnp.pad(vec, (0, padded - features)), g * width, width)

    token_f = tokens_x.astype(f32)
    norm_one = layer_norm_forward(token_f, gain_one, bias_one)[0].astype(bf16)
    bias_qkv = jnp.concatenate(
        [head_slice(bias_query), jnp.zeros((width,), f32), head_slice(bias_value)]
    )
    qkv = (product(norm_one, w_qkv, 1, 0) + bias_qkv).astype(bf16)
    ctx_mine, log_total = attention_forward(qkv, shift, length, heads)
    ctx_all = plane_gather(ctx_mine, g, rows)
    ctx_all = ctx_all.reshape(padded, members * rows)

    _, c_bit, _ = plane_bits()
    (
        norm_two, hidden_b, grad_pre_b, second_far, second_near, out_far, out_near, own_mid, units,
    ) = unit_pass(
        ctx_all, w_out, tokens_x, cot_x, up_mine, down_mine,
        jnp.stack([gain_two, bias_two, bias_out], 0), bias_up[None], rows,
    )

    def owner_send(blocks):
        return [
            lax.ppermute(
                lax.dynamic_index_in_dim(blocks, (z + d) % nz, 0, False),
                "z",
                [(i, (i + d) % nz) for i in range(nz)],
            )
            for d in range(1, nz)
        ]

    def owner_total(blocks, received):
        total = lax.dynamic_index_in_dim(blocks, z, 0, False).astype(f32)
        for piece in received:
            total = total + piece.astype(f32)
        return total


    second_far = swap(second_far, c_bit)
    up_local = product(grad_pre_b, norm_two, 0, 0).reshape(nz, unit_piece, features)
    down_local = product(hidden_b, cot_x, 0, 0).reshape(nz, unit_piece, features)
    mlp_local = jnp.concatenate([up_local.astype(bf16), down_local.astype(bf16)], 1)
    second_far, mlp_local = lax.optimization_barrier((second_far, mlp_local))
    mlp_got = owner_send(mlp_local)
    grad_second = plane_sum(second_near, second_far)
    _, xhat_two, rstd_two = layer_norm_forward(own_mid, gain_two, bias_two)
    cot_f = own_cot.astype(f32)
    grad_resid = cot_f + layer_norm_backward(grad_second, gain_two, xhat_two, rstd_two)
    grad_resid_x = plane_gather(grad_resid.astype(bf16)).reshape(members * rows, features)

    w_out_heads = lax.dynamic_slice_in_dim(
        jnp.pad(w_out, ((0, padded - features), (0, 0))), g * width, width, 0
    )
    out_far, _ = lax.optimization_barrier((out_far, grad_resid_x))
    out_far = swap(out_far, c_bit)
    first_far, first_near, qkv_local, qkv_sums = attention_backward(
        qkv, grad_resid_x, norm_one, w_out_heads, w_qkv, log_total, shift, length, heads
    )
    first_far = swap(first_far, c_bit)
    qkv_local = qkv_local.reshape(nzz, members, attn_piece, 3 * width).transpose(1, 0, 2, 3)
    qkv_local = qkv_local.reshape(members, nzz * attn_piece, 3 * width)
    qkv_moved = lax.all_to_all(qkv_local, PLANE, 0, 0, tiled=True)
    ctx_rows = ctx_all[:features].reshape(nzz, members, attn_piece, members * rows)
    ctx_rows = lax.dynamic_slice_in_dim(ctx_rows, g, 1, 1)
    ctx_rows = ctx_rows.reshape(nzz * attn_piece, members * rows)
    out_local = product(ctx_rows, grad_resid_x, 1, 0).astype(bf16)
    grad_first = plane_sum(first_near, first_far)
    _, xhat_one, rstd_one = layer_norm_forward(own_tokens.astype(f32), gain_one, bias_one)
    block_input_gradient = grad_resid + layer_norm_backward(
        grad_first, gain_one, xhat_one, rstd_one
    )

    if nzz == 1:
        attn_local = unpack_heads(qkv_moved, out_local, heads)
    else:
        qkv_moved = qkv_moved.reshape(members, nzz * attn_piece, 3, width).transpose(2, 1, 0, 3)
        qkv_moved = qkv_moved.reshape(3, nzz * attn_piece, padded)[:, :, :features]
        attn_local = jnp.concatenate([qkv_moved, out_local[None]], 0)
    attn_local = attn_local.reshape(nz, attn_piece, features)
    attn_got = owner_send(attn_local)
    attn_grad = owner_total(attn_local, attn_got)
    mlp_sum = owner_total(mlp_local, mlp_got)
    up_grad = mlp_sum[:unit_piece].T
    down_grad = mlp_sum[unit_piece:]

    block_out = own_mid + plane_sum(out_near, out_far) + bias_down

    qkv_total = jnp.sum(qkv_sums[:, 0], axis=0)

    def place_heads(vec):
        return lax.dynamic_update_slice(jnp.zeros((padded,), f32), vec, (g * width,))[:features]

    unit_sums = units[0].reshape(nz, 1, unit_piece)
    unit_sums = lax.dynamic_update_slice(
        jnp.zeros((nz, members, unit_piece), f32), unit_sums, (0, g, 0)
    ).reshape(features, 4)
    vector_rows = jnp.stack(
        [
            jnp.sum(grad_first * xhat_one, axis=0),
            jnp.sum(grad_first, axis=0),
            jnp.sum(grad_second * xhat_two, axis=0),
            jnp.sum(grad_second, axis=0),
            place_heads(qkv_total[:width]),
            place_heads(qkv_total[2 * width :]),
            jnp.sum(grad_resid, axis=0),
            jnp.sum(cot_f, axis=0),
        ],
        0,
    )
    vector_local = jnp.concatenate([vector_rows.T, unit_sums], axis=1)
    vector_local, _ = lax.optimization_barrier((vector_local, qkv_moved))
    vector_moved = lax.all_to_all(
        vector_local.reshape(nz * members, vec_piece), ("z",) + PLANE, 0, 0, tiled=True
    )
    vector_grad = jnp.sum(vector_moved, axis=0)

    attn_new, attn_moments_new = adam_update(attn_weight, attn_moments, attn_grad, decay_rate)
    up_new, up_moments_new = adam_update(up_weight, up_moments, up_grad, decay_rate)
    down_new, down_moments_new = adam_update(down_weight, down_moments, down_grad, decay_rate)
    vector_new, vector_moments_new = adam_update(vectors, vector_moments, vector_grad, 0.0)
    return (
        block_out.reshape(seq_count, rows, features),
        block_input_gradient.reshape(seq_count, rows, features),
        attn_grad,
        up_grad,
        down_grad,
        vector_grad,
        attn_new,
        up_new,
        down_new,
        vector_new,
        attn_moments_new,
        up_moments_new,
        down_moments_new,
        vector_moments_new,
    )


def solution(mesh):
    n_data, n_ctx = mesh.shape["dp"], mesh.shape["ctx"]
    fine = Mesh(mesh.devices.reshape(n_data // 4, 2, 2, n_ctx), ("z", "x", "c", "ctx"))
    data = ("z", "x", "c")
    every = ("z", "x", "c", "ctx")
    rows_spec = P(data, "ctx", None)
    in_specs = (
        rows_spec,
        P(every, None),
        P(None, every),
        P(every, None),
        P(every),
        P(None, every, None),
        P(None, None, every),
        P(None, every, None),
        P(None, every),
        rows_spec,
    )
    out_specs = (
        rows_spec,
        rows_spec,
        P(every, None),
        P(None, every),
        P(every, None),
        P(every),
        P(every, None),
        P(None, every),
        P(every, None),
        P(every),
        P(None, every, None),
        P(None, None, every),
        P(None, every, None),
        P(None, every),
    )

    return jax.shard_map(body, mesh=fine, in_specs=in_specs, out_specs=out_specs, check_vma=False)
```
